32 devices in a mesh: blk: 8 (over y, x, core), batch: 4 (over z).
Axes of the slice: x: 2, y: 2, z: 4, core: 2. Of those that a mesh axis runs over, the one named last changes fastest.
Arguments:
- query_base: bfloat16 [32, 36864], P(('batch', 'blk')), may hold values from -14 to 14
- query_latent: bfloat16 [32, 1536], P(('batch', 'blk')), may hold values from -6 to 6
- tenant_ids: int32 [32], P('batch'), may hold values from 0 to 3
- adapter_qa: bfloat16 [4, 1536, 16], replicated, may hold values from -0.15625 to 0.15625
- adapter_qb: bfloat16 [4, 16, 36864], replicated, may hold values from -0.29882812 to 0.29882812
- prefix_cache: bfloat16 [32768, 576], P('blk'), may hold values from -6 to 6
- prefix_mask: int32 [32, 256], P('batch', 'blk'), may hold values 0 or 1
- suffix_cache: bfloat16 [32, 4096, 576], P(('batch', 'blk')), may hold values from -6 to 6
- suffix_blocks: int32 [8, 4], P('blk'), may hold values from 1 to 32, 40 in all within a row
- new_latent: bfloat16 [32, 576], P(('batch', 'blk')), may hold values from -6 to 6
- value_up: bfloat16 [64, 512, 128], P('blk'), may hold values from -0.25 to 0.25
- out_weight: bfloat16 [8192, 7168], P('blk'), may hold values from -0.0625 to 0.0625
- adapter_oa: bfloat16 [4, 8192, 16], P(None, 'blk'), may hold values from -0.0625 to 0.0625
- adapter_ob: bfloat16 [4, 16, 7168], replicated, may hold values from -1.5 to 1.5
Outputs:
- attention_out: bfloat16 [32, 7168], P(('batch', 'blk'))
The draws below stay inside these ranges and needn't reach their ends.
Inputs may be any that keep to these rules, and one draw needn't show every extreme that they name: `suffix_blocks`: each row holds 40 blocks in all, and its largest entry is exactly 32.
All inputs are finite; a program needn't handle non-finite values. No bound on the sum of `prefix_mask` on one device may be relied on, other than what follows from the above.
Results may differ from the reference program's by a relative error of at most 0.025.
Values may be sent and summed in bfloat16 or wider, within the bound.
A program may use at most 128 MiB of HBM per device.

```python
import math
import jax
import jax.numpy as jnp
import numpy as np
from jax import lax

D = 7168
QL = 1536
H = 64
LAT = 512
VH = 128
QK = 192
RANK = 16
TEN = 4
BLOCK = 128
REQ_DEV = 1
SB_AVG = 10
SB_MAX = 32
KV = 576
PBLK = 256
PTOK = 32768
REQ = 32
COLUMN = 4
SUF = 4096
N_BLK = 8
N_BATCH = 4


def draw_prefix_cache(key, part):
    own_key = jax.random.fold_in(key, 11)
    values = jnp.clip(jax.random.normal(own_key, (PTOK, KV), jnp.float32), -6.0, 6.0)
    return values.astype(jnp.bfloat16)


def draw_query_base(key, part):
    own_key = jax.random.fold_in(key, 13)
    values = jnp.clip(0.5 * jax.random.normal(own_key, (REQ, H, KV), jnp.float32), -3.0, 3.0)
    return values.reshape(REQ, H * KV).astype(jnp.bfloat16)


def touch_ends(array, key, smallest, largest):
    place = [jax.random.randint(jax.random.fold_in(key, axis), (), 0, length) for axis, length in enumerate(array.shape)]
    widest = array.shape.index(max(array.shape))
    next_to = place[:widest] + [(place[widest] + 1) % array.shape[widest]] + place[widest + 1:]
    return array.at[tuple(place)].set(smallest).at[tuple(next_to)].set(largest)


def block_scale(rng, extent, split, least, high):
    def one(position, blocks):
        steps = jax.random.uniform(jax.random.fold_in(jax.random.fold_in(rng, 6), position), (blocks,), jnp.float32, least / len(split), high / len(split))
        return jnp.repeat(jnp.exp(steps), extent[position] // blocks).reshape((-1,) + (1,) * (len(extent) - position - 1))

    gain = one(*split[0])
    for cut in split[1:]:
        gain = gain * one(*cut)
    return gain


def length_profile(count, total, reach, skew):
    loads = [(1 << 20) // math.isqrt(rank ** skew) + 1 for rank in range(2, count + 1)]
    surplus, counts = total - reach - (count - 1), [1] * (count - 1)
    while surplus > 0:
        candidates = [i for i in range(count - 1) if counts[i] < reach]
        whole, budget = sum([loads[i] for i in candidates]), surplus
        for i in candidates:
            more = min(reach - counts[i], max(1, budget * loads[i] // whole), surplus)
            counts[i] = counts[i] + more
            surplus = surplus - more
    return np.array([reach] + counts)


def uneven_parts(key, number_of, total, reach, skew):
    if number_of == 2:
        one = jax.random.randint(key, (), max(1, total - reach), min(reach, total - 1) + 1)
        return jnp.stack([one, total - one])
    sizes = jnp.asarray(length_profile(number_of, total, reach, skew), jnp.int32)
    couples = (number_of - 1) // 2
    donor, receiver = sizes[1:1 + 2 * couples:2], sizes[2:2 + 2 * couples:2]
    room = jnp.minimum(donor - 1, reach - receiver)
    moved = jax.random.randint(jax.random.fold_in(key, 1), (couples,), 0, 1 << 20) % (room + 1)
    sizes = sizes.at[1:1 + 2 * couples:2].set(donor - moved).at[2:2 + 2 * couples:2].set(receiver + moved)
    return sizes[jax.random.permutation(jax.random.fold_in(key, 2), number_of)]


def gaussian(rng, shape, width, bound, pieces=(), kind=jnp.bfloat16):
    level = block_scale(rng, shape, pieces, -0.22, 0.18) if pieces else 1.0
    entries = jax.random.normal(rng, shape, jnp.float32) * width * level
    return jnp.minimum(jnp.maximum(entries, -bound), bound).astype(kind)


def setup_inputs(seed: int = 0) -> dict:
    streams_of = jax.random.split(jax.random.key(seed), 15)
    query_base = draw_query_base(jax.random.fold_in(streams_of[14], 71), 0)
    query_latent = gaussian(streams_of[1], (REQ, QL), 1.0, 6.0, ((0, 32),))
    tenant_ids = touch_ends(jax.random.randint(streams_of[2], (REQ,), 0, TEN), jax.random.fold_in(streams_of[2], 1), 0, TEN - 1).astype(jnp.int32)
    adapter_qa = gaussian(streams_of[3], (TEN, QL, RANK), QL ** -0.5, 0.15625)
    adapter_qb = gaussian(streams_of[4], (TEN, RANK, H * KV), 0.05, 0.29882812)
    prefix_cache = draw_prefix_cache(jax.random.fold_in(streams_of[14], 71), 0)
    prefix_mask = touch_ends((jax.random.randint(streams_of[6], (REQ, PBLK), 0, 6) < 1).astype(jnp.int32), jax.random.fold_in(streams_of[6], 1), 0, 1)
    suffix_cache = gaussian(streams_of[7], (REQ, SUF, KV), 1.0, 6.0, ((0, 32),))
    suffix_blocks = jax.vmap(lambda own: uneven_parts(own, COLUMN, COLUMN * SB_AVG, SB_MAX, 2))(jax.random.split(streams_of[8], N_BLK)).reshape((N_BLK, COLUMN)).astype(jnp.int32)
    new_latent = gaussian(streams_of[9], (REQ, KV), 1.0, 6.0, ((0, 32),))
    value_up = gaussian(streams_of[10], (H, LAT, VH), LAT ** -0.5, 0.25, ((0, 8),))
    out_weight = gaussian(streams_of[11], (H * VH, D), (H * VH) ** -0.5, 0.0625, ((0, 8),))
    adapter_oa = gaussian(streams_of[12], (TEN, H * VH, RANK), (H * VH) ** -0.5, 0.0625, ((1, 8),))
    adapter_ob = gaussian(streams_of[13], (TEN, RANK, D), 0.25, 1.5)
    return dict(query_base=query_base, query_latent=query_latent, tenant_ids=tenant_ids, adapter_qa=adapter_qa, adapter_qb=adapter_qb, prefix_cache=prefix_cache, prefix_mask=prefix_mask, suffix_cache=suffix_cache, suffix_blocks=suffix_blocks, new_latent=new_latent, value_up=value_up, out_weight=out_weight, adapter_oa=adapter_oa, adapter_ob=adapter_ob)


def request_lengths(suffix_blocks):
    layout = suffix_blocks.reshape(N_BLK, N_BATCH, REQ_DEV)
    return jnp.transpose(layout, (1, 0, 2)).reshape(REQ)


def reference(query_base, query_latent, tenant_ids, adapter_qa, adapter_qb, prefix_cache, prefix_mask, suffix_cache, suffix_blocks, new_latent, value_up, out_weight, adapter_oa, adapter_ob):
    score_scale = QK ** -0.5
    delta_query = jnp.zeros((REQ, H * KV), jnp.float32)
    for tenant in range(TEN):
        low_rank = jnp.dot(query_latent, adapter_qa[tenant], preferred_element_type=jnp.float32).astype(jnp.bfloat16)
        added = jnp.dot(low_rank, adapter_qb[tenant], preferred_element_type=jnp.float32)
        delta_query = jnp.where((tenant_ids == tenant)[:, None], added, delta_query)
    query = (query_base.astype(jnp.float32) + delta_query).astype(jnp.bfloat16).reshape(REQ, H, KV)
    lengths = request_lengths(suffix_blocks)
    prefix_values = prefix_cache[:, :LAT]
    contract = (((1,), (1,)), ((), ()))

    def attend(item):
        queries, mask_row, private, length, fresh = item
        token_live = jnp.repeat(mask_row > 0, BLOCK)
        pre_scores = lax.dot_general(queries, prefix_cache, contract, preferred_element_type=jnp.float32) * score_scale
        pre_scores = jnp.where(token_live[None, :], pre_scores, -jnp.inf)
        suf_scores = lax.dot_general(queries, private, contract, preferred_element_type=jnp.float32) * score_scale
        suf_live = jnp.arange(SUF, dtype=jnp.int32) < length * BLOCK
        suf_scores = jnp.where(suf_live[None, :], suf_scores, -jnp.inf)
        new_scores = jnp.dot(queries, fresh, preferred_element_type=jnp.float32) * score_scale
        peak = jnp.maximum(jnp.maximum(jnp.max(pre_scores, axis=1), jnp.max(suf_scores, axis=1)), new_scores)
        pre_weight = jnp.exp(pre_scores - peak[:, None])
        suf_weight = jnp.exp(suf_scores - peak[:, None])
        new_weight = jnp.exp(new_scores - peak)
        total = jnp.sum(pre_weight, axis=1) + jnp.sum(suf_weight, axis=1) + new_weight
        summed = jnp.dot(pre_weight.astype(jnp.bfloat16), prefix_values, preferred_element_type=jnp.float32)
        summed = summed + jnp.dot(suf_weight.astype(jnp.bfloat16), private[:, :LAT], preferred_element_type=jnp.float32)
        summed = summed + new_weight.astype(jnp.bfloat16).astype(jnp.float32)[:, None] * fresh[:LAT].astype(jnp.float32)[None, :]
        return (summed / total[:, None]).astype(jnp.bfloat16)

    context = lax.map(attend, (query, prefix_mask, suffix_cache, lengths, new_latent))
    head_out = jnp.einsum('rhl,hlv->rhv', context.astype(jnp.float32), value_up.astype(jnp.float32))
    head_out = head_out.astype(jnp.bfloat16).reshape(REQ, H * VH)
    projected = jnp.dot(head_out, out_weight, preferred_element_type=jnp.float32)
    delta_out = jnp.zeros((REQ, D), jnp.float32)
    for tenant in range(TEN):
        low_rank = jnp.dot(head_out, adapter_oa[tenant], preferred_element_type=jnp.float32)
        added = jnp.dot(low_rank, adapter_ob[tenant].astype(jnp.float32), precision=lax.Precision.HIGHEST)
        delta_out = jnp.where((tenant_ids == tenant)[:, None], added, delta_out)
    return (projected + delta_out).astype(jnp.bfloat16)
```

```python
import functools
import math

import jax
import jax.numpy as jnp
from jax import lax
from jax.experimental import pallas as pl
from jax.experimental.pallas import tpu as pltpu
from jax.sharding import PartitionSpec as P

D = 7168
H = 64
LAT = 512
VH = 128
QK = 192
RANK = 16
BLOCK = 128
KV = 576
PAIR = 2 * KV
LANES = 128
DEAD = -1e30
FLOOR = -1e25
WIDE = 640
STEP = 512
STEP2 = 1024
GROUPS = 2
VTILES = LAT // LANES
PARTS = 8
OTILES = D // PARTS // LANES
OCHUNKS = ((0, 3), (3, 5), (5, 7))
SCALE = QK ** (-0.5) * math.log2(math.e)
F32 = jnp.float32
BF16 = jnp.bfloat16
NT = (((1,), (1,)), ((), ()))


def split3(x):
    hi = x.astype(BF16).astype(F32)
    rest = x - hi
    mid = rest.astype(BF16).astype(F32)
    return hi, mid, rest - mid


def scores_pass(queries, keys, bias, scores, peak):
    rows = queries.shape[0]
    for c in range(keys.shape[1] // STEP):
        span = slice(c * STEP, (c + 1) * STEP)
        block = jnp.concatenate([keys[:, span], bias[:, span]], axis=0)
        got = jnp.dot(queries, block, preferred_element_type=F32)
        scores[:rows, span] = got
        for t in range(STEP // LANES):
            peak = jnp.maximum(peak, got[:, t * LANES : (t + 1) * LANES])
    return jnp.max(peak, axis=1, keepdims=True) * SCALE


def values_pass(peak, keys, scores):
    rows = peak.shape[0]
    total = jnp.zeros((rows, LANES), F32)
    sums = jnp.zeros((rows, LAT), F32)
    for c in range(keys.shape[1] // STEP2):
        span = slice(c * STEP2, (c + 1) * STEP2)
        weights = jnp.exp2(scores[:rows, span] * SCALE - peak)
        for t in range(STEP2 // LANES):
            total = total + weights[:, t * LANES : (t + 1) * LANES]
        sums = sums + lax.dot_general(weights.astype(BF16), keys[:LAT, span], NT, preferred_element_type=F32)
    return jnp.sum(total, axis=1, keepdims=True), sums


def kernel(
    n,
    tenant_hbm, length_hbm, base_hbm, latent_hbm, qa_hbm, qb_hbm, prefix_hbm, mask_hbm, suffix_hbm, new_hbm,
    up_hbm, weight_hbm, oa_hbm, ob_hbm,
    out_ref,
    tenant_ref, length_ref, base_ref, latent_ref, mask_ref, new_ref,
    qa, qb, prefix, suffix, up, weight, oa, ob,
    queries, prefix_bias, suffix_bias, scores, own_sums, own_stats, row_stats, sums_scr,
    send, recv, ctx_scr, row_scr, out_send, out_recv,
    small_sem, qb_sem, load_sem, q_send, q_recv, p_send, p_recv, o_send, o_recv,
):
    me = lax.axis_index("blk")
    bits = n.bit_length() - 1
    heads_here = H // n
    heads_group = heads_here // GROUPS
    pairs_group = heads_group // 2
    group_rows = H // GROUPS
    blocks = group_rows // 16

    def peer(k):
        total = 0
        for b in range(bits):
            total = total + lax.rem(lax.div(me, 1 << b) + (k >> b & 1), 2) * (1 << b)
        return total

    peers = [peer(k) for k in range(n)]
    barrier = pltpu.get_barrier_semaphore()
    for k in range(1, n):
        pl.semaphore_signal(barrier, inc=1, device_id={"blk": peers[k]}, device_id_type=pl.DeviceIdType.MESH)

    small = [
        pltpu.make_async_copy(src, dst, small_sem.at[i])
        for i, (src, dst) in enumerate(
            [(latent_hbm, latent_ref), (tenant_hbm, tenant_ref), (qa_hbm, qa), (base_hbm, base_ref),
             (mask_hbm, mask_ref), (length_hbm, length_ref), (new_hbm, new_ref)]
        )
    ]
    span_q = heads_group * KV

    def first_column(g, d):
        return (d * heads_here + g * heads_group) * KV

    qb_loads = [
        [pltpu.make_async_copy(
            qb_hbm.at[:, :, first_column(g, d) : first_column(g, d) + span_q], qb.at[g, d], qb_sem.at[g, d])
         for d in range(n)]
        for g in range(GROUPS)
    ]
    loads = [
        pltpu.make_async_copy(src, dst, load_sem.at[i])
        for i, (src, dst) in enumerate(
            [(suffix_hbm.at[0], suffix), (prefix_hbm, prefix),
             (up_hbm, up), (oa_hbm, oa), (ob_hbm, ob), (weight_hbm, weight)])
    ]
    suffix_load, prefix_load, late_loads = loads[0], loads[1], loads[2:]
    for load in small + qb_loads[0] + qb_loads[1]:
        load.start()

    for i in range(3):
        small[i].wait()
    own_tenant = tenant_ref[me]
    latent = jnp.broadcast_to(latent_ref[...].astype(F32), (16, latent_ref.shape[1])).astype(BF16)
    tenants = qa.shape[0]
    ranks = tenants * RANK
    lane_tenant = lax.broadcasted_iota(jnp.int32, (16, ranks), 1) // RANK
    low = lax.dot_general(latent, qa[...].reshape(ranks, qa.shape[2]), NT, preferred_element_type=F32)
    low_spread = jnp.where(lane_tenant == own_tenant, low, 0.0).astype(BF16)
    row_id = lax.broadcasted_iota(jnp.int32, (8, PAIR), 0)
    odd_row = lax.broadcasted_iota(jnp.int32, (group_rows, KV), 0) % heads_group >= pairs_group
    pick = (lax.broadcasted_iota(jnp.int32, (group_rows, WIDE - KV), 1) == me).astype(F32)
    small[3].wait()
    suffix_load.start()
    q_copies = {}

    def send_query(g, k, target, to):
        copy = pltpu.make_async_remote_copy(
            src_ref=queries.at[g, peers[k]], dst_ref=queries.at[g, peers[k]],
            send_sem=q_send.at[g, target], recv_sem=q_recv.at[g, target],
            device_id={"blk": peers[to]}, device_id_type=pl.DeviceIdType.MESH)
        copy.start()
        q_copies[g, target] = copy

    def forward(g, k):
        q_copies[g, k].wait_recv()
        send_query(g, k, k + 1, 1)

    for g in range(GROUPS):
        tiles = [jnp.zeros((8, PAIR), F32) for _ in range(group_rows // 8)]
        for d in range(n):
            qb_loads[g][d].wait()
            up_map = qb[g, d].reshape(ranks, span_q)
            full = jnp.dot(low_spread, up_map, preferred_element_type=F32)[:8]
            full = full + base_ref[:, first_column(g, d) : first_column(g, d) + span_q].astype(F32)
            for q in range(pairs_group):
                row = d * heads_group + q
                mask = (row_id == row % 8) | (row_id == row % 8 + pairs_group)
                tiles[row // 8] = jnp.where(mask, full[:, q * PAIR : (q + 1) * PAIR], tiles[row // 8])
        pairs = jnp.concatenate(tiles, axis=0)
        queries[g, me] = jnp.concatenate([jnp.where(odd_row, pairs[:, KV:], pairs[:, :KV]), pick], axis=1).astype(BF16)
        if g == 0:
            pl.semaphore_wait(barrier, n - 1)
        for k in list(range(2, n, 2)) + [1]:
            send_query(g, 0, k, k)
        if g == 0:
            prefix_load.start()
    for load in late_loads:
        load.start()

    for i in range(4, 7):
        small[i].wait()
    length = length_ref[0, lax.axis_index("batch")] * BLOCK
    for c in range(suffix.shape[1] // STEP):
        token = lax.broadcasted_iota(jnp.int32, (WIDE - KV, STEP), 1) + c * STEP
        suffix_bias[:, c * STEP : (c + 1) * STEP] = jnp.where(token < length, 0.0, DEAD).astype(BF16)
    dead = jnp.where(mask_ref[...] > 0, 0.0, DEAD).astype(F32)
    rest = jnp.zeros((WIDE - KV - n, BLOCK), F32)
    for b in range(mask_ref.shape[1]):
        prefix_bias[:, b * BLOCK : (b + 1) * BLOCK] = jnp.concatenate(
            [jnp.broadcast_to(dead[:, b : b + 1], (n, BLOCK)), rest], axis=0).astype(BF16)

    own = jnp.concatenate([queries[g, me] for g in range(GROUPS)], axis=0)
    fresh_key = new_ref[...].astype(F32)
    new_score = jnp.sum(own[:, :KV].astype(F32) * fresh_key, axis=1, keepdims=True)
    suffix_load.wait()
    peak = scores_pass(own, suffix, suffix_bias, scores, jnp.broadcast_to(new_score, (H, LANES)))
    for k in range(2, n, 2):
        forward(0, k)
    total, sums = values_pass(peak, suffix, scores)
    new_weight = jnp.exp2(new_score * SCALE - peak)
    own_stats[0] = jnp.broadcast_to(peak, (H, LANES))
    own_stats[1] = jnp.broadcast_to(total + new_weight, (H, LANES))
    own_sums[...] = sums + new_weight * fresh_key[:, :LAT]

    rows = n * group_rows
    mine = pl.ds(pl.multiple_of(me * group_rows, group_rows), group_rows)
    lane = lax.broadcasted_iota(jnp.int32, (rows, LANES), 1)
    p_copies = []
    prefix_load.wait()
    for g in range(GROUPS):
        for k in range(1, n, 2):
            q_copies[g, k].wait_recv()
        own_rows = slice(g * group_rows, (g + 1) * group_rows)
        row_stats[0] = jnp.full((rows, LANES), FLOOR, F32)
        row_stats[0, mine, :] = own_stats[0, own_rows, :] * (1.0 / SCALE)
        group_queries = queries[g].reshape(rows, WIDE)
        peak = scores_pass(group_queries, prefix, prefix_bias, scores, row_stats[0])
        if g + 1 < GROUPS:
            for k in range(2, n, 2):
                forward(g + 1, k)
        else:
            for copy in q_copies.values():
                copy.wait_send()
        row_stats[0] = jnp.broadcast_to(peak, (rows, LANES))
        keep = jnp.exp2(own_stats[0, own_rows, :] - row_stats[0, mine, :])
        total, sums = values_pass(peak, prefix, scores)
        row_stats[1] = jnp.broadcast_to(total, (rows, LANES))
        row_stats[1, mine, :] = row_stats[1, mine, :] + own_stats[1, own_rows, :] * keep
        stats = jnp.zeros((rows, LANES), F32)
        for i, piece in enumerate(split3(row_stats[0]) + split3(row_stats[1])):
            stats = jnp.where(lane % 8 == i, piece, stats)
        for lt in range(VTILES):
            sums_scr[lt] = sums[:, lt * LANES : (lt + 1) * LANES]
            spot = slice(lt * LANES, (lt + 1) * LANES)
            sums_scr[lt, mine, :] = sums_scr[lt, mine, :] + own_sums[own_rows, spot] * keep

        def gather(x, d):
            return jnp.concatenate(
                [x[r * group_rows + d * heads_group : r * group_rows + (d + 1) * heads_group] for r in range(n)], axis=0)

        for d in range(n):
            block = gather(stats, d)
            packed = block[:16]
            for b in range(1, blocks):
                packed = jnp.where(lane[:16] // 8 == b, block[b * 16 : (b + 1) * 16], packed)
            send[g, d, VTILES * blocks] = packed.astype(BF16)
        for lt in range(VTILES):
            part = sums_scr[lt]
            for d in range(n):
                block = gather(part, d).astype(BF16)
                for b in range(blocks):
                    send[g, d, lt * blocks + b] = block[b * 16 : (b + 1) * 16]
        for k in range(n - 1, 0, -1):
            copy = pltpu.make_async_remote_copy(
                src_ref=send.at[g, peers[k]], dst_ref=recv.at[g, k],
                send_sem=p_send.at[g, k], recv_sem=p_recv.at[g, k],
                device_id={"blk": peers[k]}, device_id_type=pl.DeviceIdType.MESH)
            copy.start()
            p_copies.append((g, copy))

    for load in late_loads:
        load.wait()
    o_copies = []
    low = jnp.zeros((n, ranks), F32)
    width = D // PARTS
    for g in range(GROUPS):
        for owner, copy in p_copies:
            if owner == g:
                copy.wait_recv()
        def tile(k, spot):
            return (send[g, me, spot] if k == 0 else recv[g, k, spot]).astype(F32)

        stats = [tile(k, VTILES * blocks) for k in range(n)]
        ms = [[s[:, b * 8 : b * 8 + 1] + s[:, b * 8 + 1 : b * 8 + 2] + s[:, b * 8 + 2 : b * 8 + 3] for s in stats]
              for b in range(blocks)]
        ls = [[s[:, b * 8 + 3 : b * 8 + 4] + s[:, b * 8 + 4 : b * 8 + 5] + s[:, b * 8 + 5 : b * 8 + 6] for s in stats]
              for b in range(blocks)]
        for b in range(blocks):
            peak = functools.reduce(jnp.maximum, ms[b])
            shares = [jnp.exp2(m - peak) for m in ms[b]]
            total = functools.reduce(jnp.add, [w * l for w, l in zip(shares, ls[b])])
            shares = [jnp.broadcast_to(w / total, (16, LANES)) for w in shares]
            for lt in range(VTILES):
                spot = lt * blocks + b
                ctx_scr[lt, b * 16 : (b + 1) * 16, :] = functools.reduce(
                    jnp.add, [shares[k] * tile(k, spot) for k in range(n)])
        heads = []
        for j in range(heads_group):
            row = j % 2 * pairs_group + j // 2
            context = jnp.concatenate(
                [ctx_scr[lt, pl.ds(row, n, stride=heads_group), :] for lt in range(VTILES)], axis=1).astype(BF16)
            heads.append(jnp.dot(context, up[g * heads_group + j], preferred_element_type=F32))
        head_out = jnp.concatenate(heads, axis=1).astype(BF16)
        span = slice(g * heads_group * VH, (g + 1) * heads_group * VH)
        low = low + lax.dot_general(
            head_out, oa[:, :, span].reshape(ranks, heads_group * VH), NT, preferred_element_type=F32)
        last = g == GROUPS - 1
        if last:
            request = lax.broadcasted_iota(jnp.int32, (n, ranks), 0)
            tenant_of = jnp.zeros((n, ranks), jnp.int32)
            for r in range(n):
                tenant_of = jnp.where(request == r, tenant_ref[r], tenant_of)
            column_tenant = lax.broadcasted_iota(jnp.int32, (n, ranks), 1) // RANK
            low = jnp.where(tenant_of == column_tenant, low, 0.0)
            low_out = jnp.concatenate(split3(low), axis=0).astype(BF16)
        for begin, end in OCHUNKS:
            picks = [slice(part * width + begin * LANES, part * width + end * LANES) for part in range(PARTS)]
            span_o = (end - begin) * LANES
            projected = jnp.dot(
                head_out, jnp.concatenate([weight[span, p] for p in picks], axis=1), preferred_element_type=F32)
            if last:
                added = jnp.dot(
                    low_out, jnp.concatenate([ob[:, :, p].reshape(ranks, span_o) for p in picks], axis=1),
                    preferred_element_type=F32)
                projected = projected + (added[:n] + added[n : 2 * n] + added[2 * n :])
            for part in range(PARTS):
                spot = slice(part * n, (part + 1) * n)
                for lt in range(begin, end):
                    first = part * span_o + (lt - begin) * LANES
                    piece = projected[:, first : first + LANES]
                    row_scr[lt, spot, :] = piece if g == 0 else row_scr[lt, spot, :] + piece
            if last:
                for k in range(n - 1, -1, -1):
                    target = out_send if k else out_recv
                    for lt in range(begin, end):
                        target[k, lt] = row_scr[lt, pl.ds(peers[k], PARTS, stride=n), :].astype(BF16)
                    if k:
                        copy = pltpu.make_async_remote_copy(
                            src_ref=out_send.at[k, begin:end], dst_ref=out_recv.at[k, begin:end],
                            send_sem=o_send.at[begin, k], recv_sem=o_recv.at[begin, k],
                            device_id={"blk": peers[k]}, device_id_type=pl.DeviceIdType.MESH)
                        copy.start()
                        o_copies.append((begin, copy))
    for _, copy in p_copies:
        copy.wait_send()
    for begin, end in OCHUNKS:
        for first, copy in o_copies:
            if first == begin:
                copy.wait_recv()
        for lt in range(begin, end):
            result = functools.reduce(jnp.add, [out_recv[k, lt].astype(F32) for k in range(n)])
            for part in range(PARTS):
                start = part * width + lt * LANES
                out_ref[:, start : start + LANES] = result[part : part + 1].astype(BF16)
    for _, copy in o_copies:
        copy.wait_send()


def on_device(
    query_base, query_latent, tenant_ids, adapter_qa, adapter_qb, prefix_cache, prefix_mask, suffix_cache,
    suffix_blocks, new_latent, value_up, out_weight, adapter_oa, adapter_ob,
):
    n = lax.axis_size("blk")
    prefix_cache = prefix_cache.T
    suffix_cache = suffix_cache.transpose(0, 2, 1)
    adapter_qa = adapter_qa.transpose(0, 2, 1)
    adapter_oa = adapter_oa.transpose(0, 2, 1)
    hbm = pl.BlockSpec(memory_space=pl.ANY)
    dma = pltpu.SemaphoreType.DMA
    slots = prefix_cache.shape[1]
    block = H // n // GROUPS * n
    out = pl.pallas_call(
        functools.partial(kernel, n),
        out_shape=pltpu.VMEM((1, D), BF16),
        in_specs=[hbm] * 14,
        out_specs=pl.BlockSpec(memory_space=pltpu.VMEM),
        scratch_shapes=[
            pltpu.SMEM(tenant_ids.shape, jnp.int32),
            pltpu.SMEM(suffix_blocks.shape, jnp.int32),
            pltpu.VMEM(query_base.shape, BF16),
            pltpu.VMEM(query_latent.shape, BF16),
            pltpu.VMEM(prefix_mask.shape, jnp.int32),
            pltpu.VMEM(new_latent.shape, BF16),
            pltpu.VMEM(adapter_qa.shape, BF16),
            pltpu.VMEM((GROUPS, n, *adapter_qb.shape[:2], H // n // GROUPS * KV), BF16),
            pltpu.VMEM(prefix_cache.shape, BF16),
            pltpu.VMEM(suffix_cache.shape[1:], BF16),
            pltpu.VMEM(value_up.shape, BF16),
            pltpu.VMEM(out_weight.shape, BF16),
            pltpu.VMEM(adapter_oa.shape, BF16),
            pltpu.VMEM(adapter_ob.shape, BF16),
            pltpu.VMEM((GROUPS, n, H // GROUPS, WIDE), BF16),
            pltpu.VMEM((WIDE - KV, slots), BF16),
            pltpu.VMEM((WIDE - KV, suffix_cache.shape[2]), BF16),
            pltpu.VMEM((max(n * H // GROUPS, H), max(slots, suffix_cache.shape[2])), F32),
            pltpu.VMEM((H, LAT), F32),
            pltpu.VMEM((2, H, LANES), F32),
            pltpu.VMEM((2, n * H // GROUPS, LANES), F32),
            pltpu.VMEM((VTILES, n * H // GROUPS, LANES), F32),
            pltpu.VMEM((GROUPS, n, block // 16 * LAT // LANES + 1, 16, LANES), BF16),
            pltpu.VMEM((GROUPS, n, block // 16 * LAT // LANES + 1, 16, LANES), BF16),
            pltpu.VMEM((LAT // LANES, block, LANES), F32),
            pltpu.VMEM((OTILES, PARTS * n, LANES), F32),
            pltpu.VMEM((n, OTILES, PARTS, LANES), BF16),
            pltpu.VMEM((n, OTILES, PARTS, LANES), BF16),
            dma((7,)), dma((GROUPS, n)), dma((6,)), dma((GROUPS, n)), dma((GROUPS, n)),
            dma((GROUPS, n)), dma((GROUPS, n)), dma((OTILES, n)), dma((OTILES, n)),
        ],
        compiler_params=pltpu.CompilerParams(
            collective_id=0, has_side_effects=True, vmem_limit_bytes=60 << 20),
    )(
        tenant_ids, suffix_blocks, query_base, query_latent, adapter_qa, adapter_qb, prefix_cache, prefix_mask,
        suffix_cache, new_latent, value_up, out_weight, adapter_oa, adapter_ob,
    )
    return out


def solution(mesh):
    placed = (
        P(("batch", "blk"), None),
        P(("batch", "blk"), None),
        P("batch"),
        P(),
        P(),
        P("blk", None),
        P("batch", "blk"),
        P(("batch", "blk"), None, None),
        P("blk", None),
        P(("batch", "blk"), None),
        P("blk", None, None),
        P("blk", None),
        P(None, "blk", None),
        P(),
    )
    return jax.shard_map(
        on_device, mesh=mesh, in_specs=placed, out_specs=P(("batch", "blk"), None), check_vma=False
    )
```

```python
import functools
import math

import jax
import jax.numpy as jnp
from jax import lax
from jax.experimental import pallas as pl
from jax.experimental.pallas import tpu as pltpu
from jax.sharding import PartitionSpec as P

D = 7168
H = 64
LAT = 512
VH = 128
QK = 192
RANK = 16
BLOCK = 128
KV = 576
PAIR = 2 * KV
LANES = 128
DEAD = -1e30
FLOOR = -1e25
WIDE = 640
STEP = 512
STEP2 = 512
GROUPS = 2
VTILES = LAT // LANES
PARTS = 8
OTILES = D // PARTS // LANES
OCHUNKS = ((0, 4), (4, 7))
SCALE = QK ** (-0.5) * math.log2(math.e)
F32 = jnp.float32
BF16 = jnp.bfloat16
NT = (((1,), (1,)), ((), ()))


def split3(x):
    hi = x.astype(BF16).astype(F32)
    rest = x - hi
    mid = rest.astype(BF16).astype(F32)
    return hi, mid, rest - mid


def scores_pass(queries, keys, bias, scores, peak):
    rows = queries.shape[0]
    for c in range(keys.shape[1] // STEP):
        span = slice(c * STEP, (c + 1) * STEP)
        block = jnp.concatenate([keys[:, span], bias[:, span]], axis=0)
        got = jnp.dot(queries, block, preferred_element_type=F32)
        scores[:rows, span] = got
        for t in range(STEP // LANES):
            peak = jnp.maximum(peak, got[:, t * LANES : (t + 1) * LANES])
    return jnp.max(peak, axis=1, keepdims=True) * SCALE


def values_pass(peak, keys, scores):
    rows = peak.shape[0]
    total = jnp.zeros((rows, LANES), F32)
    sums = jnp.zeros((rows, LAT), F32)
    for c in range(keys.shape[1] // STEP2):
        span = slice(c * STEP2, (c + 1) * STEP2)
        weights = jnp.exp2(scores[:rows, span] * SCALE - peak)
        for t in range(STEP2 // LANES):
            total = total + weights[:, t * LANES : (t + 1) * LANES]
        sums = sums + lax.dot_general(weights.astype(BF16), keys[:LAT, span], NT, preferred_element_type=F32)
    return jnp.sum(total, axis=1, keepdims=True), sums


def kernel(
    n,
    tenant_hbm, length_hbm, base_hbm, latent_hbm, qa_hbm, qb_hbm, prefix_hbm, mask_hbm, suffix_hbm, new_hbm,
    up_hbm, weight_hbm, oa_hbm, ob_hbm,
    out_ref,
    tenant_ref, length_ref, base_ref, latent_ref, mask_ref, new_ref,
    qa, qb, prefix, suffix, up, weight, oa, ob,
    queries, prefix_bias, suffix_bias, scores, own_sums, own_stats, row_stats, sums_scr,
    send, recv, ctx_scr, row_scr, out_send, out_recv,
    small_sem, qb_sem, load_sem, q_send, q_recv, p_send, p_recv, o_send, o_recv,
):
    me = lax.axis_index("blk")
    bits = n.bit_length() - 1
    heads_here = H // n
    heads_group = heads_here // GROUPS
    pairs_group = heads_group // 2
    group_rows = H // GROUPS
    blocks = group_rows // 16

    def peer(k):
        total = 0
        for b in range(bits):
            total = total + lax.rem(lax.div(me, 1 << b) + (k >> b & 1), 2) * (1 << b)
        return total

    peers = [peer(k) for k in range(n)]
    barrier = pltpu.get_barrier_semaphore()
    for k in range(1, n):
        pl.semaphore_signal(barrier, inc=1, device_id={"blk": peers[k]}, device_id_type=pl.DeviceIdType.MESH)

    small = [
        pltpu.make_async_copy(src, dst, small_sem.at[i])
        for i, (src, dst) in enumerate(
            [(latent_hbm, latent_ref), (tenant_hbm, tenant_ref), (qa_hbm, qa), (base_hbm, base_ref),
             (mask_hbm, mask_ref), (length_hbm, length_ref), (new_hbm, new_ref)]
        )
    ]
    span_q = heads_group * KV

    def first_column(g, d):
        return (d * heads_here + g * heads_group) * KV

    qb_loads = [
        [pltpu.make_async_copy(
            qb_hbm.at[:, :, first_column(g, d) : first_column(g, d) + span_q],
            qb.at[g, :, :, d * span_q : (d + 1) * span_q], qb_sem.at[g, d])
         for d in range(n)]
        for g in range(GROUPS)
    ]
    loads = [
        pltpu.make_async_copy(src, dst, load_sem.at[i])
        for i, (src, dst) in enumerate(
            [(suffix_hbm.at[0], suffix), (prefix_hbm, prefix),
             (up_hbm, up), (oa_hbm, oa), (ob_hbm, ob), (weight_hbm, weight)])
    ]
    suffix_load, prefix_load, late_loads = loads[0], loads[1], loads[2:]
    for load in small + qb_loads[0] + qb_loads[1]:
        load.start()

    for i in range(3):
        small[i].wait()
    own_tenant = tenant_ref[me]
    latent = jnp.broadcast_to(latent_ref[...].astype(F32), (16, latent_ref.shape[1])).astype(BF16)
    tenants = qa.shape[0]
    ranks = tenants * RANK
    lane_tenant = lax.broadcasted_iota(jnp.int32, (16, ranks), 1) // RANK
    low = lax.dot_general(latent, qa[...].reshape(ranks, qa.shape[2]), NT, preferred_element_type=F32)
    low_spread = jnp.where(lane_tenant == own_tenant, low, 0.0).astype(BF16)
    row_id = lax.broadcasted_iota(jnp.int32, (8, PAIR), 0)
    odd_row = lax.broadcasted_iota(jnp.int32, (group_rows, KV), 0) % heads_group >= pairs_group
    pick = (lax.broadcasted_iota(jnp.int32, (group_rows, WIDE - KV), 1) == me).astype(F32)
    small[3].wait()
    suffix_load.start()
    q_copies = {}

    def send_query(g, k, target, to):
        copy = pltpu.make_async_remote_copy(
            src_ref=queries.at[g, peers[k]], dst_ref=queries.at[g, peers[k]],
            send_sem=q_send.at[g, target], recv_sem=q_recv.at[g, target],
            device_id={"blk": peers[to]}, device_id_type=pl.DeviceIdType.MESH)
        copy.start()
        q_copies[g, target] = copy

    def send_queries(g):
        for k in list(range(2, n, 2)) + [1]:
            send_query(g, 0, k, k)

    def forward(g, k):
        q_copies[g, k].wait_recv()
        send_query(g, k, k + 1, 1)

    for i in range(4, 7):
        small[i].wait()
    length = length_ref[0, lax.axis_index("batch")] * BLOCK
    for c in range(suffix.shape[1] // STEP):
        token = lax.broadcasted_iota(jnp.int32, (WIDE - KV, STEP), 1) + c * STEP
        suffix_bias[:, c * STEP : (c + 1) * STEP] = jnp.where(token < length, 0.0, DEAD).astype(BF16)
    dead = jnp.where(mask_ref[...] > 0, 0.0, DEAD).astype(F32)
    rest = jnp.zeros((WIDE - KV - n, BLOCK), F32)
    for b in range(mask_ref.shape[1]):
        prefix_bias[:, b * BLOCK : (b + 1) * BLOCK] = jnp.concatenate(
            [jnp.broadcast_to(dead[:, b : b + 1], (n, BLOCK)), rest], axis=0).astype(BF16)

    for g in range(GROUPS):
        for d in range(n):
            qb_loads[g][d].wait()
        delta = jnp.dot(low_spread, qb[g].reshape(ranks, n * span_q), preferred_element_type=F32)[:8]
        tiles = [jnp.zeros((8, PAIR), F32) for _ in range(group_rows // 8)]
        for p in range(group_rows // 2):
            d, q = p // pairs_group, p % pairs_group
            column = first_column(g, d) + q * PAIR
            full = delta[:, p * PAIR : (p + 1) * PAIR] + base_ref[:, column : column + PAIR].astype(F32)
            row = d * heads_group + q
            mask = (row_id == row % 8) | (row_id == row % 8 + pairs_group)
            tiles[row // 8] = jnp.where(mask, full, tiles[row // 8])
        pairs = jnp.concatenate(tiles, axis=0)
        queries[g, me] = jnp.concatenate([jnp.where(odd_row, pairs[:, KV:], pairs[:, :KV]), pick], axis=1).astype(BF16)
        if g == 0:
            pl.semaphore_wait(barrier, n - 1)
            send_queries(g)
            prefix_load.start()

    own = jnp.concatenate([queries[g, me] for g in range(GROUPS)], axis=0)
    fresh_key = new_ref[...].astype(F32)
    new_score = jnp.sum(own[:, :KV].astype(F32) * fresh_key, axis=1, keepdims=True)
    suffix_load.wait()
    peak = scores_pass(own, suffix, suffix_bias, scores, jnp.broadcast_to(new_score, (H, LANES)))
    for g in range(1, GROUPS):
        send_queries(g)
    total, sums = values_pass(peak, suffix, scores)
    new_weight = jnp.exp2(new_score * SCALE - peak)
    own_stats[0] = jnp.broadcast_to(peak, (H, LANES))
    own_stats[1] = jnp.broadcast_to(total + new_weight, (H, LANES))
    own_sums[...] = sums + new_weight * fresh_key[:, :LAT]

    rows = n * group_rows
    mine = pl.ds(pl.multiple_of(me * group_rows, group_rows), group_rows)
    lane = lax.broadcasted_iota(jnp.int32, (rows, LANES), 1)
    p_copies = []
    for k in range(2, n, 2):
        forward(0, k)
    prefix_load.wait()
    for load in late_loads:
        load.start()
    for g in range(GROUPS):
        for k in range(1, n, 2):
            q_copies[g, k].wait_recv()
        own_rows = slice(g * group_rows, (g + 1) * group_rows)
        row_stats[0] = jnp.full((rows, LANES), FLOOR, F32)
        row_stats[0, mine, :] = own_stats[0, own_rows, :] * (1.0 / SCALE)
        group_queries = queries[g].reshape(rows, WIDE)
        peak = scores_pass(group_queries, prefix, prefix_bias, scores, row_stats[0])
        if g + 1 < GROUPS:
            for k in range(2, n, 2):
                forward(g + 1, k)
        else:
            for copy in q_copies.values():
                copy.wait_send()
        row_stats[0] = jnp.broadcast_to(peak, (rows, LANES))
        keep = jnp.exp2(own_stats[0, own_rows, :] - row_stats[0, mine, :])
        total, sums = values_pass(peak, prefix, scores)
        row_stats[1] = jnp.broadcast_to(total, (rows, LANES))
        row_stats[1, mine, :] = row_stats[1, mine, :] + own_stats[1, own_rows, :] * keep
        stats = jnp.zeros((rows, LANES), F32)
        for i, piece in enumerate(split3(row_stats[0]) + split3(row_stats[1])):
            stats = jnp.where(lane % 8 == i, piece, stats)
        for lt in range(VTILES):
            sums_scr[lt] = sums[:, lt * LANES : (lt + 1) * LANES]
            spot = slice(lt * LANES, (lt + 1) * LANES)
            sums_scr[lt, mine, :] = sums_scr[lt, mine, :] + own_sums[own_rows, spot] * keep

        def gather(x, d):
            return jnp.concatenate(
                [x[r * group_rows + d * heads_group : r * group_rows + (d + 1) * heads_group] for r in range(n)], axis=0)

        for d in range(n):
            block = gather(stats, d)
            packed = block[:16]
            for b in range(1, blocks):
                packed = jnp.where(lane[:16] // 8 == b, block[b * 16 : (b + 1) * 16], packed)
            send[g, d, VTILES * blocks] = packed.astype(BF16)
        for lt in range(VTILES):
            part = sums_scr[lt]
            for d in range(n):
                block = gather(part, d).astype(BF16)
                for b in range(blocks):
                    send[g, d, lt * blocks + b] = block[b * 16 : (b + 1) * 16]
        for k in range(n - 1, 0, -1):
            copy = pltpu.make_async_remote_copy(
                src_ref=send.at[g, peers[k]], dst_ref=recv.at[g, k],
                send_sem=p_send.at[g, k], recv_sem=p_recv.at[g, k],
                device_id={"blk": peers[k]}, device_id_type=pl.DeviceIdType.MESH)
            copy.start()
            p_copies.append((g, copy))

    for load in late_loads:
        load.wait()
    o_copies = []
    low = jnp.zeros((n, ranks), F32)
    width = D // PARTS
    for g in range(GROUPS):
        for owner, copy in p_copies:
            if owner == g:
                copy.wait_recv()
        def tile(k, spot):
            return (send[g, me, spot] if k == 0 else recv[g, k, spot]).astype(F32)

        stats = [tile(k, VTILES * blocks) for k in range(n)]
        ms = [[s[:, b * 8 : b * 8 + 1] + s[:, b * 8 + 1 : b * 8 + 2] + s[:, b * 8 + 2 : b * 8 + 3] for s in stats]
              for b in range(blocks)]
        ls = [[s[:, b * 8 + 3 : b * 8 + 4] + s[:, b * 8 + 4 : b * 8 + 5] + s[:, b * 8 + 5 : b * 8 + 6] for s in stats]
              for b in range(blocks)]
        for b in range(blocks):
            peak = functools.reduce(jnp.maximum, ms[b])
            shares = [jnp.exp2(m - peak) for m in ms[b]]
            total = functools.reduce(jnp.add, [w * l for w, l in zip(shares, ls[b])])
            shares = [jnp.broadcast_to(w / total, (16, LANES)) for w in shares]
            for lt in range(VTILES):
                spot = lt * blocks + b
                ctx_scr[lt, b * 16 : (b + 1) * 16, :] = functools.reduce(
                    jnp.add, [shares[k] * tile(k, spot) for k in range(n)])
        heads = []
        for j in range(heads_group):
            row = j % 2 * pairs_group + j // 2
            context = jnp.concatenate(
                [ctx_scr[lt, pl.ds(row, n, stride=heads_group), :] for lt in range(VTILES)], axis=1).astype(BF16)
            heads.append(jnp.dot(context, up[g * heads_group + j], preferred_element_type=F32))
        head_out = jnp.concatenate(heads, axis=1).astype(BF16)
        span = slice(g * heads_group * VH, (g + 1) * heads_group * VH)
        low = low + lax.dot_general(
            head_out, oa[:, :, span].reshape(ranks, heads_group * VH), NT, preferred_element_type=F32)
        last = g == GROUPS - 1
        if last:
            request = lax.broadcasted_iota(jnp.int32, (n, ranks), 0)
            tenant_of = jnp.zeros((n, ranks), jnp.int32)
            for r in range(n):
                tenant_of = jnp.where(request == r, tenant_ref[r], tenant_of)
            column_tenant = lax.broadcasted_iota(jnp.int32, (n, ranks), 1) // RANK
            low = jnp.where(tenant_of == column_tenant, low, 0.0)
            low_out = jnp.concatenate(split3(low), axis=0).astype(BF16)
        for begin, end in OCHUNKS:
            picks = [slice(part * width + begin * LANES, part * width + end * LANES) for part in range(PARTS)]
            span_o = (end - begin) * LANES
            projected = jnp.dot(
                head_out, jnp.concatenate([weight[span, p] for p in picks], axis=1), preferred_element_type=F32)
            if last:
                added = jnp.dot(
                    low_out, jnp.concatenate([ob[:, :, p].reshape(ranks, span_o) for p in picks], axis=1),
                    preferred_element_type=F32)
                projected = projected + (added[:n] + added[n : 2 * n] + added[2 * n :])
            for part in range(PARTS):
                spot = slice(part * n, (part + 1) * n)
                for lt in range(begin, end):
                    first = part * span_o + (lt - begin) * LANES
                    piece = projected[:, first : first + LANES]
                    row_scr[lt, spot, :] = piece if g == 0 else row_scr[lt, spot, :] + piece
            if last:
                for k in range(n - 1, -1, -1):
                    target = out_send if k else out_recv
                    for lt in range(begin, end):
                        target[k, lt] = row_scr[lt, pl.ds(peers[k], PARTS, stride=n), :].astype(BF16)
                    if k:
                        copy = pltpu.make_async_remote_copy(
                            src_ref=out_send.at[k, begin:end], dst_ref=out_recv.at[k, begin:end],
                            send_sem=o_send.at[begin, k], recv_sem=o_recv.at[begin, k],
                            device_id={"blk": peers[k]}, device_id_type=pl.DeviceIdType.MESH)
                        copy.start()
                        o_copies.append((begin, copy))
    for _, copy in p_copies:
        copy.wait_send()
    for begin, end in OCHUNKS:
        for first, copy in o_copies:
            if first == begin:
                copy.wait_recv()
        for lt in range(begin, end):
            result = functools.reduce(jnp.add, [out_recv[k, lt].astype(F32) for k in range(n)])
            for part in range(PARTS):
                start = part * width + lt * LANES
                out_ref[:, start : start + LANES] = result[part : part + 1].astype(BF16)
    for _, copy in o_copies:
        copy.wait_send()


def on_device(
    query_base, query_latent, tenant_ids, adapter_qa, adapter_qb, prefix_cache, prefix_mask, suffix_cache,
    suffix_blocks, new_latent, value_up, out_weight, adapter_oa, adapter_ob,
):
    n = lax.axis_size("blk")
    prefix_cache = prefix_cache.T
    suffix_cache = suffix_cache.transpose(0, 2, 1)
    adapter_qa = adapter_qa.transpose(0, 2, 1)
    adapter_oa = adapter_oa.transpose(0, 2, 1)
    hbm = pl.BlockSpec(memory_space=pl.ANY)
    dma = pltpu.SemaphoreType.DMA
    slots = prefix_cache.shape[1]
    block = H // n // GROUPS * n
    out = pl.pallas_call(
        functools.partial(kernel, n),
        out_shape=pltpu.VMEM((1, D), BF16),
        in_specs=[hbm] * 14,
        out_specs=pl.BlockSpec(memory_space=pltpu.VMEM),
        scratch_shapes=[
            pltpu.SMEM(tenant_ids.shape, jnp.int32),
            pltpu.SMEM(suffix_blocks.shape, jnp.int32),
            pltpu.VMEM(query_base.shape, BF16),
            pltpu.VMEM(query_latent.shape, BF16),
            pltpu.VMEM(prefix_mask.shape, jnp.int32),
            pltpu.VMEM(new_latent.shape, BF16),
            pltpu.VMEM(adapter_qa.shape, BF16),
            pltpu.VMEM((GROUPS, *adapter_qb.shape[:2], H // GROUPS * KV), BF16),
            pltpu.VMEM(prefix_cache.shape, BF16),
            pltpu.VMEM(suffix_cache.shape[1:], BF16),
            pltpu.VMEM(value_up.shape, BF16),
            pltpu.VMEM(out_weight.shape, BF16),
            pltpu.VMEM(adapter_oa.shape, BF16),
            pltpu.VMEM(adapter_ob.shape, BF16),
            pltpu.VMEM((GROUPS, n, H // GROUPS, WIDE), BF16),
            pltpu.VMEM((WIDE - KV, slots), BF16),
            pltpu.VMEM((WIDE - KV, suffix_cache.shape[2]), BF16),
            pltpu.VMEM((max(n * H // GROUPS, H), max(slots, suffix_cache.shape[2])), F32),
            pltpu.VMEM((H, LAT), F32),
            pltpu.VMEM((2, H, LANES), F32),
            pltpu.VMEM((2, n * H // GROUPS, LANES), F32),
            pltpu.VMEM((VTILES, n * H // GROUPS, LANES), F32),
            pltpu.VMEM((GROUPS, n, block // 16 * LAT // LANES + 1, 16, LANES), BF16),
            pltpu.VMEM((GROUPS, n, block // 16 * LAT // LANES + 1, 16, LANES), BF16),
            pltpu.VMEM((LAT // LANES, block, LANES), F32),
            pltpu.VMEM((OTILES, PARTS * n, LANES), F32),
            pltpu.VMEM((n, OTILES, PARTS, LANES), BF16),
            pltpu.VMEM((n, OTILES, PARTS, LANES), BF16),
            dma((7,)), dma((GROUPS, n)), dma((6,)), dma((GROUPS, n)), dma((GROUPS, n)),
            dma((GROUPS, n)), dma((GROUPS, n)), dma((OTILES, n)), dma((OTILES, n)),
        ],
        compiler_params=pltpu.CompilerParams(
            collective_id=0, has_side_effects=True, vmem_limit_bytes=60 << 20),
    )(
        tenant_ids, suffix_blocks, query_base, query_latent, adapter_qa, adapter_qb, prefix_cache, prefix_mask,
        suffix_cache, new_latent, value_up, out_weight, adapter_oa, adapter_ob,
    )
    return out


def solution(mesh):
    placed = (
        P(("batch", "blk"), None),
        P(("batch", "blk"), None),
        P("batch"),
        P(),
        P(),
        P("blk", None),
        P("batch", "blk"),
        P(("batch", "blk"), None, None),
        P("blk", None),
        P(("batch", "blk"), None),
        P("blk", None, None),
        P("blk", None),
        P(None, "blk", None),
        P(),
    )
    return jax.shard_map(
        on_device, mesh=mesh, in_specs=placed, out_specs=P(("batch", "blk"), None), check_vma=False
    )
```
